32 devices in a mesh: pts: 8 (over y, x, core), lst: 4 (over z).
Axes of the slice: x: 2, y: 2, z: 4, core: 2. Of those that a mesh axis runs over, the one named last changes fastest.
Arguments:
- tower_out: bfloat16 [16384, 1024], P('pts', 'lst'), may hold values from -6 to 6
- projection: bfloat16 [1024, 256], P('lst'), may hold values from -1 to 1
- centroids: bfloat16 [16384, 256], P('lst'), may hold values from -6 to 6
Outputs:
- new_centroids: float32 [16384, 256], P(('lst', 'pts'))
- row_log: float32 [16384], P('pts')
The draws below stay inside these ranges and needn't reach their ends.
All inputs are finite; a program needn't handle non-finite values.
Results may differ from the reference program's by a relative error of at most 0.0045.
Values may be sent and summed in bfloat16 or wider, within the bound.
A program may use at most 64 MiB of HBM per device.

```python
import math
import jax
import jax.numpy as jnp
from jax import lax

DIN = 1024
DP = 256
KC = 16384
ITERS = 3
NPTS = 16384


strength = 0.35


planted = 1.0


def plus_minus(seeded, total_count):
    return (jax.random.randint(seeded, (total_count,), 0, 2) * 2 - 1).astype(jnp.float32)


def tower_axis(key):
    return plus_minus(jax.random.fold_in(jax.random.fold_in(key, 101), 1), DIN)


def list_axis(key):
    return plus_minus(jax.random.fold_in(jax.random.fold_in(key, 101), 2), DP)


def group_signs(seeded, total_count, lowest, highest):
    border = jax.random.randint(seeded, (), lowest, highest)
    return jnp.where(jnp.arange(total_count) < border, 1.0, -1.0).astype(jnp.float32)


def draw_tower_out(key, part):
    tower_dir = tower_axis(key)
    point_sign = group_signs(jax.random.fold_in(key, 12), NPTS, 65 * NPTS // 100, 80 * NPTS // 100 + 1)
    jitter = jnp.clip(jax.random.normal(jax.random.fold_in(key, 11), (NPTS, DIN), jnp.float32), -5.5, 5.5)
    values = jitter + strength * point_sign[:, None] * tower_dir[None, :]
    return values.astype(jnp.bfloat16)


def draw_projection(key, part):
    tower_dir = tower_axis(key)
    list_dir = list_axis(key)
    dense = jnp.clip(jax.random.normal(jax.random.fold_in(key, 21), (DIN, DP), jnp.float32), -6.0, 6.0)
    values = dense * (1.0 / math.sqrt(DIN)) + planted / DIN * tower_dir[:, None] * list_dir[None, :]
    return values.astype(jnp.bfloat16)


def draw_centroids(key, part):
    list_dir = list_axis(key)
    list_sign = group_signs(jax.random.fold_in(key, 32), KC, 20 * KC // 100, 35 * KC // 100 + 1)
    jitter = jnp.clip(jax.random.normal(jax.random.fold_in(key, 31), (KC, DP), jnp.float32), -5.5, 5.5)
    values = jitter + strength * list_sign[:, None] * list_dir[None, :]
    return values.astype(jnp.bfloat16)


def setup_inputs(seed: int = 0) -> dict:
    key_list = jax.random.split(jax.random.key(seed), 4)
    tower_out = draw_tower_out(jax.random.fold_in(key_list[3], 71), 0)
    projection = draw_projection(jax.random.fold_in(key_list[3], 71), 0)
    centroids = draw_centroids(jax.random.fold_in(key_list[3], 71), 0)
    return dict(tower_out=tower_out, projection=projection, centroids=centroids)


temper = 0.05

def rms_norm(values):
    return values * lax.rsqrt(lax.optimization_barrier(jnp.mean(values * values, axis=-1, keepdims=True)) + 1e-06)

def energy(zblock, unit_lists):
    scores = lax.dot_general(zblock, unit_lists, (((1,), (1,)), ((), ())), preferred_element_type=jnp.float32)
    return jnp.exp(scores / (DP * temper) - 1.0 / temper)

def reference(tower_out, projection, centroids):
    hidden = jnp.dot(tower_out, projection, preferred_element_type=jnp.float32)
    normed = rms_norm(hidden).astype(jnp.bfloat16)
    unit_lists = rms_norm(centroids.astype(jnp.float32)).astype(jnp.bfloat16)
    block_rows = min(512, NPTS)
    block_count = NPTS // block_rows
    blocks = normed.reshape(block_count, block_rows, DP)
    balance = NPTS / KC
    row_scale = jnp.ones((NPTS,), jnp.float32)
    col_scale = jnp.ones((KC,), jnp.float32)
    for sweep in range(ITERS):

        def column_step(running, inputs):
            zblock, scale_blk = inputs
            return (running + lax.optimization_barrier(jnp.sum(energy(zblock, unit_lists) * scale_blk[:, None], axis=0)), None)
        column_sum = lax.scan(column_step, jnp.zeros((KC,), jnp.float32), (blocks, row_scale.reshape(block_count, block_rows)))[0]
        col_scale = balance / column_sum

        def row_step(zblock, scales=col_scale):
            return lax.optimization_barrier(jnp.sum(energy(zblock, unit_lists) * scales[None, :], axis=1))
        row_sum = lax.map(row_step, blocks).reshape(NPTS)
        row_scale = 1.0 / row_sum

    def update_step(running, inputs):
        zblock, scale_blk = inputs
        weights = (scale_blk[:, None] * energy(zblock, unit_lists) * col_scale[None, :]).astype(jnp.bfloat16)
        sums_part = lax.dot_general(weights, zblock, (((0,), (0,)), ((), ())), preferred_element_type=jnp.float32)
        return (running + sums_part, None)
    list_sums = lax.scan(update_step, jnp.zeros((KC, DP), jnp.float32), (blocks, row_scale.reshape(block_count, block_rows)))[0]
    return (rms_norm(list_sums), jnp.log(row_scale))
```

```python
import functools
import math

import jax
import jax.numpy as jnp
from jax import lax
from jax.experimental import pallas as pl
from jax.experimental.pallas import tpu as pltpu
from jax.sharding import PartitionSpec as P

ITERS = 3
temper = 0.05
LANES = 128
MESH = pl.DeviceIdType.MESH
F32 = jnp.float32
BF16 = jnp.bfloat16


def rms_norm(values):
    return values * lax.rsqrt(jnp.mean(values * values, axis=-1, keepdims=True) + 1e-06)


def column_of(row, rows):
    return jnp.broadcast_to(row, (rows, LANES)).T


def kernel(
    npts,
    nlst,
    tower,
    proj,
    cent,
    out,
    row_log,
    energy,
    unit,
    full,
    pfull,
    normed,
    lane_sums,
    col_sums,
    row_sums,
    col_wide,
    scaled,
    pair_send,
    pair_recv,
    chip_send,
    chip_recv,
    mine,
    t_send,
    t_recv,
    p_send,
    p_recv,
    n_send,
    n_recv,
    c_send,
    c_recv,
    r_send,
    r_recv,
    x_send,
    x_recv,
    y_send,
    y_recv,
):
    pts = lax.axis_index("pts")
    lst = lax.axis_index("lst")
    lists, dp = cent.shape
    points = tower.shape[0]
    share = points // nlst
    own = lists // npts
    chips = npts // 2
    core = pts % 2
    chip = pts // 2
    balance = (points * npts) / (lists * nlst)
    list_blocks = lists // LANES
    point_blocks = points // LANES

    barrier = pltpu.get_barrier_semaphore()
    for d in range(1, nlst):
        pl.semaphore_signal(
            barrier, inc=1, device_id={"lst": (lst + d) % nlst}, device_id_type=MESH
        )
    for d in range(1, npts):
        pl.semaphore_signal(
            barrier, inc=1, device_id={"pts": (pts + d) % npts}, device_id_type=MESH
        )
    pl.semaphore_wait(barrier, nlst + npts - 2)

    pending = []

    def send(src, dst, send_sem, recv_sem, axis, target):
        copy = pltpu.make_async_remote_copy(
            src_ref=src,
            dst_ref=dst,
            send_sem=send_sem,
            recv_sem=recv_sem,
            device_id={axis: target},
            device_id_type=MESH,
        )
        copy.start()
        pending.append(copy)
        return copy

    p_copies = [
        send(proj, pfull.at[d], p_send.at[d], p_recv.at[d], "lst", (lst + d) % nlst)
        for d in range(1, nlst)
    ]
    t_copies = []
    for d in range(1, nlst):
        z = (lst + d) % nlst
        t_copies.append(
            send(
                tower.at[pl.ds(pl.multiple_of(z * share, share), share)],
                full.at[d],
                t_send.at[d],
                t_recv.at[d],
                "lst",
                z,
            )
        )

    unit_rows = min(256, lists)

    @pl.loop(0, lists // unit_rows)
    def _(b):
        rows = pl.ds(pl.multiple_of(b * unit_rows, unit_rows), unit_rows)
        unit[rows, :] = rms_norm(cent[rows, :].astype(F32)).astype(BF16)
        lane_sums[rows, :] = jnp.zeros((unit_rows, LANES), F32)

    hidden = jnp.dot(
        tower[pl.ds(pl.multiple_of(lst * share, share), share), :],
        proj[...],
        preferred_element_type=F32,
    )
    for d in range(1, nlst):
        p_copies[d - 1].wait_recv()
        t_copies[d - 1].wait_recv()
        hidden += jnp.dot(full[d], pfull[d], preferred_element_type=F32)
    normed[0] = rms_norm(hidden).astype(BF16)
    n_copies = [
        send(normed.at[0], normed.at[d], n_send.at[d], n_recv.at[d], "lst", (lst + d) % nlst)
        for d in range(1, nlst)
    ]

    log2e = 1.0 / math.log(2.0)
    gain = log2e / (dp * temper)
    shift = -log2e / temper
    e_rows = min(256, lists)
    for d in range(nlst):
        if d:
            n_copies[d - 1].wait_recv()

        @pl.loop(0, lists // e_rows)
        def _(b, d=d):
            rows = pl.ds(pl.multiple_of(b * e_rows, e_rows), e_rows)
            sums = lane_sums[rows, :]
            step = min(256, share)
            for k in range(share // step):
                scores = lax.dot_general(
                    unit[rows, :],
                    normed[d, k * step : (k + 1) * step, :],
                    (((1,), (1,)), ((), ())),
                    preferred_element_type=F32,
                )
                block = jnp.exp2(scores * gain + shift)
                at = d * share + k * step
                energy[rows, at : at + step] = block
                for m in range(step // LANES):
                    sums += block[:, m * LANES : (m + 1) * LANES]
            lane_sums[rows, :] = sums

    def lane_dense(sums):
        return jnp.sum(sums.T, axis=0, keepdims=True)

    row_scale = None
    for sweep in range(ITERS):

        @pl.loop(0, list_blocks)
        def _(b, sweep=sweep, row_scale=row_scale):
            rows = pl.ds(pl.multiple_of(b * LANES, LANES), LANES)
            if sweep == 0:
                sums = lane_sums[rows, :]
            else:
                sums = energy[rows, 0:LANES] * row_scale[:, 0:LANES]
                for m in range(1, point_blocks):
                    lanes = slice(m * LANES, (m + 1) * LANES)
                    sums += energy[rows, lanes] * row_scale[:, lanes]
            col_sums[sweep, 0, pl.ds(b, 1), :] = lane_dense(sums)

        copies = [
            send(
                col_sums.at[sweep, 0],
                col_sums.at[sweep, d],
                c_send.at[sweep, d],
                c_recv.at[sweep, d],
                "pts",
                (pts + d) % npts,
            )
            for d in range(1, npts)
        ]
        for copy in copies:
            copy.wait_recv()
        total = col_sums[sweep, 0]
        for d in range(1, npts):
            total += col_sums[sweep, d]
        lane_sums[0:list_blocks, :] = balance / total

        def row_step(b, acc):
            rows = pl.ds(pl.multiple_of(b * LANES, LANES), LANES)
            wide = column_of(lane_sums[pl.ds(b, 1), :], LANES)
            if sweep == ITERS - 1:
                col_wide[rows, :] = wide
            parts = []
            for m in range(point_blocks):
                lanes = slice(m * LANES, (m + 1) * LANES)
                term = energy[rows, lanes] * wide
                parts.append(acc[m] + jnp.sum(term.reshape(LANES // 8, 8, LANES), axis=0))
            return tuple(parts)

        acc = lax.fori_loop(
            0,
            list_blocks,
            row_step,
            tuple(jnp.zeros((8, LANES), F32) for _ in range(point_blocks)),
        )
        per_slot = share // LANES
        for d in range(nlst):
            z = (lst + nlst - d) % nlst
            parts = [
                jnp.sum(acc[d * per_slot + m], axis=0, keepdims=True) for m in range(per_slot)
            ]
            row_sums[sweep, 0, pl.ds(z, 1), :] = jnp.concatenate(parts, axis=1)
        copies = [
            send(
                row_sums.at[sweep, 0],
                row_sums.at[sweep, d],
                r_send.at[sweep, d],
                r_recv.at[sweep, d],
                "lst",
                (lst + d) % nlst,
            )
            for d in range(1, nlst)
        ]
        for copy in copies:
            copy.wait_recv()
        total = row_sums[sweep, 0]
        for d in range(1, nlst):
            total += row_sums[sweep, d]
        scale = 1.0 / total
        row_log[...] = scale
        row_scale = jnp.concatenate(
            [row_log[pl.ds((lst + nlst - d) % nlst, 1), :] for d in range(nlst)], axis=1
        )
    row_log[...] = jnp.log(scale)

    for m in range(point_blocks):
        d, k = divmod(m * LANES, share)
        wide = column_of(row_scale[:, m * LANES : (m + 1) * LANES], LANES)
        block = normed[d, k : k + LANES, :].astype(F32)
        for h in range(dp // LANES):
            lanes = slice(h * LANES, (h + 1) * LANES)
            scaled[m * LANES : (m + 1) * LANES, lanes] = (block[:, lanes] * wide).astype(BF16)

    tile = min(256, own)

    def partial_sums(owner, store):
        @pl.loop(0, own // tile)
        def _(t):
            rows = pl.ds(pl.multiple_of(owner * own + t * tile, tile), tile)
            store(
                pl.ds(pl.multiple_of(t * tile, tile), tile),
                jnp.dot(energy[rows, :].astype(BF16), scaled[...], preferred_element_type=F32),
            )

    partner = pts + 1 - 2 * core
    x_copies = []
    order = [d % chips for d in range(1, chips + 1)]
    for d in order:

        def to_pair(rows, values, d=d):
            pair_send[d, rows, :] = values.astype(BF16)

        partial_sums(((chip + d) % chips) * 2 + 1 - core, to_pair)
        x_copies.append(
            send(pair_send.at[d], pair_recv.at[d], x_send.at[d], x_recv.at[d], "pts", partner)
        )
    y_copies = []
    for n, d in enumerate(order):

        def to_mine(rows, values):
            mine[rows, :] = values

        owner = ((chip + d) % chips) * 2 + core
        partial_sums(owner, to_mine)
        x_copies[n].wait_recv()
        pair = mine[...] + pair_recv[d].astype(F32)
        if d:
            chip_send[d] = pair.astype(BF16)
            y_copies.append(
                send(chip_send.at[d], chip_recv.at[d], y_send.at[d], y_recv.at[d], "pts", owner)
            )
        else:
            mine[...] = pair
    for copy in y_copies:
        copy.wait_recv()
    sums = mine[...]
    for d in range(1, chips):
        sums += chip_recv[d].astype(F32)
    wide = col_wide[pl.ds(pl.multiple_of(pts * own, own), own), :]
    sums = sums * jnp.concatenate([wide] * (dp // LANES), axis=1)
    out[...] = rms_norm(sums)
    for copy in pending:
        copy.wait_send()


def on_device(npts, nlst, tower_out, projection, centroids):
    points = tower_out.shape[0]
    lists, dp = centroids.shape
    feats = tower_out.shape[1]
    share = points // nlst
    own = lists // npts
    chips = npts // 2
    vmem = pl.BlockSpec(memory_space=pltpu.VMEM)
    sem = pltpu.SemaphoreType.DMA
    centers, row_log = pl.pallas_call(
        functools.partial(kernel, npts, nlst),
        out_shape=(
            jax.ShapeDtypeStruct((own, dp), F32),
            jax.ShapeDtypeStruct((nlst, share), F32),
        ),
        in_specs=[vmem] * 3,
        out_specs=(vmem, vmem),
        scratch_shapes=[
            pltpu.VMEM((lists, points), F32),
            pltpu.VMEM((lists, dp), BF16),
            pltpu.VMEM((nlst, share, feats), BF16),
            pltpu.VMEM((nlst, feats, dp), BF16),
            pltpu.VMEM((nlst, share, dp), BF16),
            pltpu.VMEM((lists, LANES), F32),
            pltpu.VMEM((ITERS, npts, lists // LANES, LANES), F32),
            pltpu.VMEM((ITERS, nlst, nlst, share), F32),
            pltpu.VMEM((lists, LANES), F32),
            pltpu.VMEM((points, dp), BF16),
            pltpu.VMEM((chips, own, dp), BF16),
            pltpu.VMEM((chips, own, dp), BF16),
            pltpu.VMEM((chips, own, dp), BF16),
            pltpu.VMEM((chips, own, dp), BF16),
            pltpu.VMEM((own, dp), F32),
            sem((nlst,)),
            sem((nlst,)),
            sem((nlst,)),
            sem((nlst,)),
            sem((nlst,)),
            sem((nlst,)),
            sem((ITERS, npts)),
            sem((ITERS, npts)),
            sem((ITERS, nlst)),
            sem((ITERS, nlst)),
            sem((chips,)),
            sem((chips,)),
            sem((chips,)),
            sem((chips,)),
        ],
        compiler_params=pltpu.CompilerParams(
            collective_id=0, has_side_effects=True, vmem_limit_bytes=64000000
        ),
    )(tower_out, projection, centroids)
    return centers, row_log.reshape(points)


def solution(mesh):
    return jax.shard_map(
        functools.partial(on_device, mesh.shape["pts"], mesh.shape["lst"]),
        mesh=mesh,
        in_specs=(P("pts", "lst"), P("lst", None), P("lst", None)),
        out_specs=(P(("lst", "pts"), None), P("pts")),
        check_vma=False,
    )
```

```python
import functools
import math

import jax
import jax.numpy as jnp
from jax import lax
from jax.experimental import pallas as pl
from jax.experimental.pallas import tpu as pltpu
from jax.sharding import PartitionSpec as P

ITERS = 3
temper = 0.05
LANES = 128
MESH = pl.DeviceIdType.MESH
F32 = jnp.float32
BF16 = jnp.bfloat16


def rms_norm(values):
    return values * lax.rsqrt(jnp.mean(values * values, axis=-1, keepdims=True) + 1e-06)


def column_of(row, rows):
    return jnp.broadcast_to(row, (rows, LANES)).T


def kernel(
    npts,
    nlst,
    chunks,
    tower,
    proj,
    cent,
    out,
    row_log,
    energy,
    unit,
    full,
    pfull,
    normed,
    lane_sums,
    col_sums,
    row_sums,
    col_wide,
    scaled,
    pair_send,
    pair_recv,
    chip_send,
    chip_recv,
    mine,
    t_send,
    t_recv,
    p_send,
    p_recv,
    q_send,
    q_recv,
    n_send,
    n_recv,
    c_send,
    c_recv,
    r_send,
    r_recv,
    x_send,
    x_recv,
    y_send,
    y_recv,
):
    pts = lax.axis_index("pts")
    lst = lax.axis_index("lst")
    lists, dp = cent.shape
    points = tower.shape[0]
    share = points // nlst
    own = lists // npts
    chips = npts // 2
    core = pts % 2
    chip = pts // 2
    balance = (points * npts) / (lists * nlst)
    list_blocks = lists // LANES
    point_blocks = points // LANES

    barrier = pltpu.get_barrier_semaphore()
    for d in range(1, nlst):
        pl.semaphore_signal(
            barrier, inc=1, device_id={"lst": (lst + d) % nlst}, device_id_type=MESH
        )
    for d in range(1, npts):
        pl.semaphore_signal(
            barrier, inc=1, device_id={"pts": (pts + d) % npts}, device_id_type=MESH
        )
    pl.semaphore_wait(barrier, nlst + npts - 2)

    pending = []

    def send(src, dst, send_sem, recv_sem, axis, target):
        copy = pltpu.make_async_remote_copy(
            src_ref=src,
            dst_ref=dst,
            send_sem=send_sem,
            recv_sem=recv_sem,
            device_id={axis: target},
            device_id_type=MESH,
        )
        copy.start()
        pending.append(copy)
        return copy

    feats = proj.shape[0]
    piece = feats // npts
    sliced = piece % 16 == 0
    if sliced:
        piece_rows = pl.ds(pl.multiple_of(pts * piece, piece), piece)
    else:
        piece_rows = pl.ds(0, feats)
    p_copies = [
        send(
            proj.at[piece_rows],
            pfull.at[d, piece_rows],
            p_send.at[d],
            p_recv.at[d],
            "lst",
            (lst + d) % nlst,
        )
        for d in range(1, nlst)
    ]
    chunk = share // chunks
    t_copies = []
    for c in range(chunks):
        for d in range(1, nlst):
            z = (lst + d) % nlst
            t_copies.append(
                send(
                    tower.at[pl.ds(pl.multiple_of(z * share + c * chunk, chunk), chunk)],
                    full.at[c, d],
                    t_send.at[c, d],
                    t_recv.at[c, d],
                    "lst",
                    z,
                )
            )
    unit_rows = min(256, lists)

    @pl.loop(0, lists // unit_rows)
    def _(b):
        rows = pl.ds(pl.multiple_of(b * unit_rows, unit_rows), unit_rows)
        unit[rows, :] = rms_norm(cent[rows, :].astype(F32)).astype(BF16)
        lane_sums[rows, :] = jnp.zeros((unit_rows, LANES), F32)

    for copy in p_copies:
        copy.wait_recv()
    if sliced:
        q_copies = [
            send(
                pfull.at[pl.ds(1, nlst - 1), piece_rows],
                pfull.at[pl.ds(1, nlst - 1), piece_rows],
                q_send.at[d],
                q_recv.at[d],
                "pts",
                (pts + d) % npts,
            )
            for d in range(1, npts)
        ]

    if sliced:
        for copy in q_copies:
            copy.wait_recv()

    def hop(c, origin, left):
        side = 0 if left else 1
        return pltpu.make_async_remote_copy(
            src_ref=normed.at[c, origin],
            dst_ref=normed.at[c, origin],
            send_sem=n_send.at[side, c, origin],
            recv_sem=n_recv.at[c, origin],
            device_id={"lst": lst - 1 if left else lst + 1},
            device_id_type=MESH,
        )

    has_left = lst > 0
    has_right = lst < nlst - 1
    for c in range(chunks):
        hidden = jnp.dot(
            tower[pl.ds(pl.multiple_of(lst * share + c * chunk, chunk), chunk), :],
            proj[...],
            preferred_element_type=F32,
        )
        for d in range(1, nlst):
            t_copies[c * (nlst - 1) + d - 1].wait_recv()
            hidden += jnp.dot(full[c, d], pfull[d], preferred_element_type=F32)
        normed[c, lst] = rms_norm(hidden).astype(BF16)

        @pl.when(has_left)
        def _(c=c):
            hop(c, lst, True).start()

        @pl.when(has_right)
        def _(c=c):
            hop(c, lst, False).start()

    log2e = 1.0 / math.log(2.0)
    gain = log2e / (dp * temper)
    shift = -log2e / temper
    e_rows = min(256, lists)
    step = min(256, chunk)

    def energy_of(c, origin):
        @pl.loop(0, lists // e_rows)
        def _(b):
            rows = pl.ds(pl.multiple_of(b * e_rows, e_rows), e_rows)
            sums = lane_sums[rows, :]
            for k in range(chunk // step):
                scores = lax.dot_general(
                    unit[rows, :],
                    normed[c, origin, k * step : (k + 1) * step, :],
                    (((1,), (1,)), ((), ())),
                    preferred_element_type=F32,
                )
                block = jnp.exp2(scores * gain + shift)
                at = pl.multiple_of(origin * share + c * chunk + k * step, step)
                energy[rows, pl.ds(at, step)] = block
                for m in range(step // LANES):
                    sums += block[:, m * LANES : (m + 1) * LANES]
            lane_sums[rows, :] = sums

    paired = jnp.minimum(lst, nlst - 1 - lst)
    for s in range(nlst):
        near = (s + 1) // 2
        far = s - paired
        in_pairs = lst - near if s % 2 else lst + near
        beyond = jnp.where(has_right & (lst < nlst - 1 - lst), lst + far, lst - far)
        origin = jnp.where(s <= 2 * paired, in_pairs, beyond) if s else lst
        for c in range(chunks):
            if s:
                hop(c, origin, True).wait_recv()

                @pl.when((origin < lst) & has_right)
                def _(c=c, origin=origin):
                    hop(c, origin, False).start()

                @pl.when((origin > lst) & has_left)
                def _(c=c, origin=origin):
                    hop(c, origin, True).start()

            energy_of(c, origin)

    for z in range(nlst):
        for c in range(chunks):

            @pl.when((z <= lst) & has_right)
            def _(c=c, z=z):
                hop(c, z, False).wait_send()

            @pl.when((z >= lst) & has_left)
            def _(c=c, z=z):
                hop(c, z, True).wait_send()

    def lane_dense(sums):
        return jnp.sum(sums.T, axis=0, keepdims=True)

    row_scale = None
    for sweep in range(ITERS):

        @pl.loop(0, list_blocks)
        def _(b, sweep=sweep, row_scale=row_scale):
            rows = pl.ds(pl.multiple_of(b * LANES, LANES), LANES)
            if sweep == 0:
                sums = lane_sums[rows, :]
            else:
                sums = energy[rows, 0:LANES] * row_scale[:, 0:LANES]
                for m in range(1, point_blocks):
                    lanes = slice(m * LANES, (m + 1) * LANES)
                    sums += energy[rows, lanes] * row_scale[:, lanes]
            col_sums[sweep, 0, pl.ds(b, 1), :] = lane_dense(sums)

        copies = [
            send(
                col_sums.at[sweep, 0],
                col_sums.at[sweep, d],
                c_send.at[sweep, d],
                c_recv.at[sweep, d],
                "pts",
                (pts + d) % npts,
            )
            for d in range(1, npts)
        ]
        for copy in copies:
            copy.wait_recv()
        total = col_sums[sweep, 0]
        for d in range(1, npts):
            total += col_sums[sweep, d]
        lane_sums[0:list_blocks, :] = balance / total

        def row_step(b, acc):
            rows = pl.ds(pl.multiple_of(b * LANES, LANES), LANES)
            wide = column_of(lane_sums[pl.ds(b, 1), :], LANES)
            if sweep == ITERS - 1:
                col_wide[rows, :] = wide
            parts = []
            for m in range(point_blocks):
                lanes = slice(m * LANES, (m + 1) * LANES)
                term = energy[rows, lanes] * wide
                parts.append(acc[m] + jnp.sum(term.reshape(LANES // 8, 8, LANES), axis=0))
            return tuple(parts)

        acc = lax.fori_loop(
            0,
            list_blocks,
            row_step,
            tuple(jnp.zeros((8, LANES), F32) for _ in range(point_blocks)),
        )
        per_slot = share // LANES
        for d in range(nlst):
            parts = [
                jnp.sum(acc[d * per_slot + m], axis=0, keepdims=True) for m in range(per_slot)
            ]
            row_sums[sweep, 0, d : d + 1, :] = jnp.concatenate(parts, axis=1)
        copies = [
            send(
                row_sums.at[sweep, 0],
                row_sums.at[sweep, d],
                r_send.at[sweep, d],
                r_recv.at[sweep, d],
                "lst",
                (lst + d) % nlst,
            )
            for d in range(1, nlst)
        ]
        for copy in copies:
            copy.wait_recv()
        total = row_sums[sweep, 0]
        for d in range(1, nlst):
            total += row_sums[sweep, d]
        scale = 1.0 / total
        row_scale = jnp.concatenate([scale[d : d + 1, :] for d in range(nlst)], axis=1)
    row_log[...] = jnp.log(scale)

    for m in range(point_blocks):
        d, k = divmod(m * LANES, share)
        wide = column_of(row_scale[:, m * LANES : (m + 1) * LANES], LANES)
        c, k = divmod(k, chunk)
        block = normed[c, d, k : k + LANES, :].astype(F32)
        for h in range(dp // LANES):
            lanes = slice(h * LANES, (h + 1) * LANES)
            scaled[m * LANES : (m + 1) * LANES, lanes] = (block[:, lanes] * wide).astype(BF16)

    tile = min(256, own)

    def partial_sums(owner, store):
        @pl.loop(0, own // tile)
        def _(t):
            rows = pl.ds(pl.multiple_of(owner * own + t * tile, tile), tile)
            store(
                pl.ds(pl.multiple_of(t * tile, tile), tile),
                jnp.dot(energy[rows, :].astype(BF16), scaled[...], preferred_element_type=F32),
            )

    partner = pts + 1 - 2 * core
    x_copies = []
    order = [d % chips for d in range(1, chips + 1)]
    for d in order:

        def to_pair(rows, values, d=d):
            pair_send[d, rows, :] = values.astype(BF16)

        partial_sums(((chip + d) % chips) * 2 + 1 - core, to_pair)
        x_copies.append(
            send(pair_send.at[d], pair_recv.at[d], x_send.at[d], x_recv.at[d], "pts", partner)
        )
    y_copies = []
    for n, d in enumerate(order):

        def to_mine(rows, values):
            mine[rows, :] = values

        owner = ((chip + d) % chips) * 2 + core
        partial_sums(owner, to_mine)
        x_copies[n].wait_recv()
        pair = mine[...] + pair_recv[d].astype(F32)
        if d:
            chip_send[d] = pair.astype(BF16)
            y_copies.append(
                send(chip_send.at[d], chip_recv.at[d], y_send.at[d], y_recv.at[d], "pts", owner)
            )
        else:
            mine[...] = pair
    for copy in y_copies:
        copy.wait_recv()
    sums = mine[...]
    for d in range(1, chips):
        sums += chip_recv[d].astype(F32)
    wide = col_wide[pl.ds(pl.multiple_of(pts * own, own), own), :]
    sums = sums * jnp.concatenate([wide] * (dp // LANES), axis=1)
    out[...] = rms_norm(sums)
    for copy in pending:
        copy.wait_send()


def on_device(npts, nlst, tower_out, projection, centroids):
    points = tower_out.shape[0]
    lists, dp = centroids.shape
    feats = tower_out.shape[1]
    share = points // nlst
    own = lists // npts
    chips = npts // 2
    chunks = 2 if share % (2 * LANES) == 0 else 1
    chunk = share // chunks
    vmem = pl.BlockSpec(memory_space=pltpu.VMEM)
    sem = pltpu.SemaphoreType.DMA
    centers, row_log = pl.pallas_call(
        functools.partial(kernel, npts, nlst, chunks),
        out_shape=(
            jax.ShapeDtypeStruct((own, dp), F32),
            jax.ShapeDtypeStruct((nlst, share), F32),
        ),
        in_specs=[vmem] * 3,
        out_specs=(vmem, vmem),
        scratch_shapes=[
            pltpu.VMEM((lists, points), F32),
            pltpu.VMEM((lists, dp), BF16),
            pltpu.VMEM((chunks, nlst, chunk, feats), BF16),
            pltpu.VMEM((nlst, feats, dp), BF16),
            pltpu.VMEM((chunks, nlst, chunk, dp), BF16),
            pltpu.VMEM((lists, LANES), F32),
            pltpu.VMEM((ITERS, npts, lists // LANES, LANES), F32),
            pltpu.VMEM((ITERS, nlst, nlst, share), F32),
            pltpu.VMEM((lists, LANES), F32),
            pltpu.VMEM((points, dp), BF16),
            pltpu.VMEM((chips, own, dp), BF16),
            pltpu.VMEM((chips, own, dp), BF16),
            pltpu.VMEM((chips, own, dp), BF16),
            pltpu.VMEM((chips, own, dp), BF16),
            pltpu.VMEM((own, dp), F32),
            sem((chunks, nlst)),
            sem((chunks, nlst)),
            sem((nlst,)),
            sem((nlst,)),
            sem((npts,)),
            sem((npts,)),
            sem((2, chunks, nlst)),
            sem((chunks, nlst)),
            sem((ITERS, npts)),
            sem((ITERS, npts)),
            sem((ITERS, nlst)),
            sem((ITERS, nlst)),
            sem((chips,)),
            sem((chips,)),
            sem((chips,)),
            sem((chips,)),
        ],
        compiler_params=pltpu.CompilerParams(
            collective_id=0, has_side_effects=True, vmem_limit_bytes=64000000
        ),
    )(tower_out, projection, centroids)
    return centers, row_log.reshape(points)


def solution(mesh):
    return jax.shard_map(
        functools.partial(on_device, mesh.shape["pts"], mesh.shape["lst"]),
        mesh=mesh,
        in_specs=(P("pts", "lst"), P("lst", None), P("lst", None)),
        out_specs=(P(("lst", "pts"), None), P("pts")),
        check_vma=False,
    )
```

```python
import functools
import math

import jax
import jax.numpy as jnp
from jax import lax
from jax.experimental import pallas as pl
from jax.experimental.pallas import tpu as pltpu
from jax.sharding import PartitionSpec as P

ITERS = 3
temper = 0.05
LANES = 128
MESH = pl.DeviceIdType.MESH
F32 = jnp.float32
BF16 = jnp.bfloat16


def rms_norm(values):
    return values * lax.rsqrt(jnp.mean(values * values, axis=-1, keepdims=True) + 1e-06)


def column_of(row, rows):
    return jnp.broadcast_to(row, (rows, LANES)).T


def kernel(
    npts,
    nlst,
    chunks,
    tower,
    proj,
    cent,
    out,
    row_log,
    energy,
    unit,
    full,
    pfull,
    normed,
    lane_sums,
    col_sums,
    row_sums,
    col_wide,
    scaled,
    pair_send,
    pair_recv,
    chip_send,
    chip_recv,
    mine,
    t_send,
    t_recv,
    p_send,
    p_recv,
    q_send,
    q_recv,
    n_send,
    n_recv,
    c_send,
    c_recv,
    r_send,
    r_recv,
    x_send,
    x_recv,
    y_send,
    y_recv,
):
    pts = lax.axis_index("pts")
    lst = lax.axis_index("lst")
    lists, dp = cent.shape
    points = tower.shape[0]
    share = points // nlst
    own = lists // npts
    chips = npts // 2
    core = pts % 2
    chip = pts // 2
    balance = (points * npts) / (lists * nlst)
    list_blocks = lists // LANES
    point_blocks = points // LANES

    barrier = pltpu.get_barrier_semaphore()
    for d in range(1, nlst):
        pl.semaphore_signal(
            barrier, inc=1, device_id={"lst": (lst + d) % nlst}, device_id_type=MESH
        )
    for d in range(1, npts):
        pl.semaphore_signal(
            barrier, inc=1, device_id={"pts": (pts + d) % npts}, device_id_type=MESH
        )
    pl.semaphore_wait(barrier, nlst + npts - 2)

    pending = []

    def send(src, dst, send_sem, recv_sem, axis, target):
        copy = pltpu.make_async_remote_copy(
            src_ref=src,
            dst_ref=dst,
            send_sem=send_sem,
            recv_sem=recv_sem,
            device_id={axis: target},
            device_id_type=MESH,
        )
        copy.start()
        pending.append(copy)
        return copy

    feats = proj.shape[0]
    piece = feats // npts
    sliced = piece % 16 == 0
    if sliced:
        piece_rows = pl.ds(pl.multiple_of(pts * piece, piece), piece)
    else:
        piece_rows = pl.ds(0, feats)
    p_copies = [
        send(
            proj.at[piece_rows],
            pfull.at[d, piece_rows],
            p_send.at[d],
            p_recv.at[d],
            "lst",
            (lst + d) % nlst,
        )
        for d in range(1, nlst)
    ]
    chunk = share // chunks
    t_copies = []
    for c in range(chunks):
        for d in range(1, nlst):
            z = (lst + d) % nlst
            t_copies.append(
                send(
                    tower.at[pl.ds(pl.multiple_of(z * share + c * chunk, chunk), chunk)],
                    full.at[c, d],
                    t_send.at[c, d],
                    t_recv.at[c, d],
                    "lst",
                    z,
                )
            )
    unit_rows = min(256, lists)

    @pl.loop(0, lists // unit_rows)
    def _(b):
        rows = pl.ds(pl.multiple_of(b * unit_rows, unit_rows), unit_rows)
        unit[rows, :] = rms_norm(cent[rows, :].astype(F32)).astype(BF16)
        lane_sums[rows, :] = jnp.zeros((unit_rows, LANES), F32)

    for copy in p_copies:
        copy.wait_recv()
    if sliced:
        q_copies = [
            send(
                pfull.at[pl.ds(1, nlst - 1), piece_rows],
                pfull.at[pl.ds(1, nlst - 1), piece_rows],
                q_send.at[d],
                q_recv.at[d],
                "pts",
                (pts + d) % npts,
            )
            for d in range(1, npts)
        ]

    if sliced:
        for copy in q_copies:
            copy.wait_recv()

    def hop(c, origin, left):
        side = 0 if left else 1
        return pltpu.make_async_remote_copy(
            src_ref=normed.at[c, origin],
            dst_ref=normed.at[c, origin],
            send_sem=n_send.at[side, c, origin],
            recv_sem=n_recv.at[c, origin],
            device_id={"lst": lst - 1 if left else lst + 1},
            device_id_type=MESH,
        )

    has_left = lst > 0
    has_right = lst < nlst - 1
    for c in range(chunks):
        hidden = jnp.dot(
            tower[pl.ds(pl.multiple_of(lst * share + c * chunk, chunk), chunk), :],
            proj[...],
            preferred_element_type=F32,
        )
        for d in range(1, nlst):
            t_copies[c * (nlst - 1) + d - 1].wait_recv()
            hidden += jnp.dot(full[c, d], pfull[d], preferred_element_type=F32)
        normed[c, lst] = rms_norm(hidden).astype(BF16)

        @pl.when(has_left)
        def _(c=c):
            hop(c, lst, True).start()

        @pl.when(has_right)
        def _(c=c):
            hop(c, lst, False).start()

    log2e = 1.0 / math.log(2.0)
    gain = log2e / (dp * temper)
    shift = -log2e / temper
    e_rows = min(1024, lists)
    step = min(256, chunk)

    def energy_of(c, origin):
        @pl.loop(0, lists // e_rows)
        def _(b):
            rows = pl.ds(pl.multiple_of(b * e_rows, e_rows), e_rows)
            sums = lane_sums[rows, :]
            for k in range(chunk // step):
                scores = lax.dot_general(
                    unit[rows, :],
                    normed[c, origin, k * step : (k + 1) * step, :],
                    (((1,), (1,)), ((), ())),
                    preferred_element_type=F32,
                )
                block = jnp.exp2(scores * gain + shift)
                at = pl.multiple_of(origin * share + c * chunk + k * step, step)
                energy[rows, pl.ds(at, step)] = block
                for m in range(step // LANES):
                    sums += block[:, m * LANES : (m + 1) * LANES]
            lane_sums[rows, :] = sums

    paired = jnp.minimum(lst, nlst - 1 - lst)
    for s in range(nlst):
        near = (s + 1) // 2
        far = s - paired
        in_pairs = lst - near if s % 2 else lst + near
        beyond = jnp.where(has_right & (lst < nlst - 1 - lst), lst + far, lst - far)
        origin = jnp.where(s <= 2 * paired, in_pairs, beyond) if s else lst
        for c in range(chunks):
            if s:
                hop(c, origin, True).wait_recv()

                @pl.when((origin < lst) & has_right)
                def _(c=c, origin=origin):
                    hop(c, origin, False).start()

                @pl.when((origin > lst) & has_left)
                def _(c=c, origin=origin):
                    hop(c, origin, True).start()

            energy_of(c, origin)

    for z in range(nlst):
        for c in range(chunks):

            @pl.when((z <= lst) & has_right)
            def _(c=c, z=z):
                hop(c, z, False).wait_send()

            @pl.when((z >= lst) & has_left)
            def _(c=c, z=z):
                hop(c, z, True).wait_send()

    def lane_dense(sums):
        return jnp.sum(sums.T, axis=0, keepdims=True)

    row_scale = None
    for sweep in range(ITERS):

        @pl.loop(0, list_blocks, unroll=2)
        def _(b, sweep=sweep, row_scale=row_scale):
            rows = pl.ds(pl.multiple_of(b * LANES, LANES), LANES)
            if sweep == 0:
                sums = lane_sums[rows, :]
            else:
                sums = energy[rows, 0:LANES] * row_scale[:, 0:LANES]
                for m in range(1, point_blocks):
                    lanes = slice(m * LANES, (m + 1) * LANES)
                    sums += energy[rows, lanes] * row_scale[:, lanes]
            col_sums[sweep, 0, pl.ds(b, 1), :] = lane_dense(sums)

        copies = [
            send(
                col_sums.at[sweep, 0],
                col_sums.at[sweep, d],
                c_send.at[sweep, d],
                c_recv.at[sweep, d],
                "pts",
                (pts + d) % npts,
            )
            for d in range(1, npts)
        ]
        for copy in copies:
            copy.wait_recv()
        total = col_sums[sweep, 0]
        for d in range(1, npts):
            total += col_sums[sweep, d]
        lane_sums[0:list_blocks, :] = balance / total

        def row_step(b, acc):
            rows = pl.ds(pl.multiple_of(b * LANES, LANES), LANES)
            wide = column_of(lane_sums[pl.ds(b, 1), :], LANES)
            if sweep == ITERS - 1:
                col_wide[rows, :] = wide
            parts = []
            for m in range(point_blocks):
                lanes = slice(m * LANES, (m + 1) * LANES)
                term = energy[rows, lanes] * wide
                parts.append(acc[m] + jnp.sum(term.reshape(LANES // 8, 8, LANES), axis=0))
            return tuple(parts)

        acc = lax.fori_loop(
            0,
            list_blocks,
            row_step,
            tuple(jnp.zeros((8, LANES), F32) for _ in range(point_blocks)),
            unroll=2,
        )
        per_slot = share // LANES
        for d in range(nlst):
            parts = [
                jnp.sum(acc[d * per_slot + m], axis=0, keepdims=True) for m in range(per_slot)
            ]
            row_sums[sweep, 0, d : d + 1, :] = jnp.concatenate(parts, axis=1)
        copies = [
            send(
                row_sums.at[sweep, 0],
                row_sums.at[sweep, d],
                r_send.at[sweep, d],
                r_recv.at[sweep, d],
                "lst",
                (lst + d) % nlst,
            )
            for d in range(1, nlst)
        ]
        for copy in copies:
            copy.wait_recv()
        total = row_sums[sweep, 0]
        for d in range(1, nlst):
            total += row_sums[sweep, d]
        scale = 1.0 / total
        row_scale = jnp.concatenate([scale[d : d + 1, :] for d in range(nlst)], axis=1)
    row_log[...] = jnp.log(scale)

    for m in range(point_blocks):
        d, k = divmod(m * LANES, share)
        wide = column_of(row_scale[:, m * LANES : (m + 1) * LANES], LANES)
        c, k = divmod(k, chunk)
        block = normed[c, d, k : k + LANES, :].astype(F32)
        for h in range(dp // LANES):
            lanes = slice(h * LANES, (h + 1) * LANES)
            scaled[m * LANES : (m + 1) * LANES, lanes] = (block[:, lanes] * wide).astype(BF16)

    tile = min(256, own)

    def partial_sums(owner, store):
        @pl.loop(0, own // tile)
        def _(t):
            rows = pl.ds(pl.multiple_of(owner * own + t * tile, tile), tile)
            store(
                pl.ds(pl.multiple_of(t * tile, tile), tile),
                jnp.dot(energy[rows, :].astype(BF16), scaled[...], preferred_element_type=F32),
            )

    partner = pts + 1 - 2 * core
    x_copies = []
    order = [d % chips for d in range(1, chips + 1)]
    for d in order:

        def to_pair(rows, values, d=d):
            pair_send[d, rows, :] = values.astype(BF16)

        partial_sums(((chip + d) % chips) * 2 + 1 - core, to_pair)
        x_copies.append(
            send(pair_send.at[d], pair_recv.at[d], x_send.at[d], x_recv.at[d], "pts", partner)
        )
    y_copies = []
    for n, d in enumerate(order):

        def to_mine(rows, values):
            mine[rows, :] = values

        owner = ((chip + d) % chips) * 2 + core
        partial_sums(owner, to_mine)
        x_copies[n].wait_recv()
        pair = mine[...] + pair_recv[d].astype(F32)
        if d:
            chip_send[d] = pair.astype(BF16)
            y_copies.append(
                send(chip_send.at[d], chip_recv.at[d], y_send.at[d], y_recv.at[d], "pts", owner)
            )
        else:
            mine[...] = pair
    for copy in y_copies:
        copy.wait_recv()
    sums = mine[...]
    for d in range(1, chips):
        sums += chip_recv[d].astype(F32)
    wide = col_wide[pl.ds(pl.multiple_of(pts * own, own), own), :]
    sums = sums * jnp.concatenate([wide] * (dp // LANES), axis=1)
    out[...] = rms_norm(sums)
    for copy in pending:
        copy.wait_send()


def on_device(npts, nlst, tower_out, projection, centroids):
    points = tower_out.shape[0]
    lists, dp = centroids.shape
    feats = tower_out.shape[1]
    share = points // nlst
    own = lists // npts
    chips = npts // 2
    chunks = 2 if share % (2 * LANES) == 0 else 1
    chunk = share // chunks
    vmem = pl.BlockSpec(memory_space=pltpu.VMEM)
    sem = pltpu.SemaphoreType.DMA
    centers, row_log = pl.pallas_call(
        functools.partial(kernel, npts, nlst, chunks),
        out_shape=(
            jax.ShapeDtypeStruct((own, dp), F32),
            jax.ShapeDtypeStruct((nlst, share), F32),
        ),
        in_specs=[vmem] * 3,
        out_specs=(vmem, vmem),
        scratch_shapes=[
            pltpu.VMEM((lists, points), F32),
            pltpu.VMEM((lists, dp), BF16),
            pltpu.VMEM((chunks, nlst, chunk, feats), BF16),
            pltpu.VMEM((nlst, feats, dp), BF16),
            pltpu.VMEM((chunks, nlst, chunk, dp), BF16),
            pltpu.VMEM((lists, LANES), F32),
            pltpu.VMEM((ITERS, npts, lists // LANES, LANES), F32),
            pltpu.VMEM((ITERS, nlst, nlst, share), F32),
            pltpu.VMEM((lists, LANES), F32),
            pltpu.VMEM((points, dp), BF16),
            pltpu.VMEM((chips, own, dp), BF16),
            pltpu.VMEM((chips, own, dp), BF16),
            pltpu.VMEM((chips, own, dp), BF16),
            pltpu.VMEM((chips, own, dp), BF16),
            pltpu.VMEM((own, dp), F32),
            sem((chunks, nlst)),
            sem((chunks, nlst)),
            sem((nlst,)),
            sem((nlst,)),
            sem((npts,)),
            sem((npts,)),
            sem((2, chunks, nlst)),
            sem((chunks, nlst)),
            sem((ITERS, npts)),
            sem((ITERS, npts)),
            sem((ITERS, nlst)),
            sem((ITERS, nlst)),
            sem((chips,)),
            sem((chips,)),
            sem((chips,)),
            sem((chips,)),
        ],
        compiler_params=pltpu.CompilerParams(
            collective_id=0, has_side_effects=True, vmem_limit_bytes=64000000
        ),
    )(tower_out, projection, centroids)
    return centers, row_log.reshape(points)


def solution(mesh):
    return jax.shard_map(
        functools.partial(on_device, mesh.shape["pts"], mesh.shape["lst"]),
        mesh=mesh,
        in_specs=(P("pts", "lst"), P("lst", None), P("lst", None)),
        out_specs=(P(("lst", "pts"), None), P("pts")),
        check_vma=False,
    )
```

```python
import functools
import math

import jax
import jax.numpy as jnp
from jax import lax
from jax.experimental import pallas as pl
from jax.experimental.pallas import tpu as pltpu
from jax.sharding import PartitionSpec as P

ITERS = 3
temper = 0.05
LANES = 128
MESH = pl.DeviceIdType.MESH
F32 = jnp.float32
BF16 = jnp.bfloat16


def rms_norm(values):
    return values * lax.rsqrt(jnp.mean(values * values, axis=-1, keepdims=True) + 1e-06)


def column_of(row, rows):
    return jnp.broadcast_to(row, (rows, LANES)).T


def kernel(
    npts,
    nlst,
    chunks,
    tower,
    proj,
    cent,
    out,
    row_log,
    energy,
    unit,
    full,
    pfull,
    normed,
    lane_sums,
    col_sums,
    row_sums,
    col_wide,
    scaled,
    pair_send,
    pair_recv,
    chip_send,
    chip_recv,
    mine,
    t_send,
    t_recv,
    p_send,
    p_recv,
    q_send,
    q_recv,
    n_send,
    n_recv,
    c_send,
    c_recv,
    r_send,
    r_recv,
    x_send,
    x_recv,
    y_send,
    y_recv,
):
    pts = lax.axis_index("pts")
    lst = lax.axis_index("lst")
    lists, dp = cent.shape
    points = tower.shape[0]
    share = points // nlst
    own = lists // npts
    chips = npts // 2
    core = pts % 2
    chip = pts // 2
    balance = (points * npts) / (lists * nlst)
    list_blocks = lists // LANES
    point_blocks = points // LANES

    barrier = pltpu.get_barrier_semaphore()
    for d in range(1, nlst):
        pl.semaphore_signal(
            barrier, inc=1, device_id={"lst": (lst + d) % nlst}, device_id_type=MESH
        )
    for d in range(1, npts):
        pl.semaphore_signal(
            barrier, inc=1, device_id={"pts": (pts + d) % npts}, device_id_type=MESH
        )
    pl.semaphore_wait(barrier, nlst + npts - 2)

    pending = []

    def send(src, dst, send_sem, recv_sem, axis, target):
        copy = pltpu.make_async_remote_copy(
            src_ref=src,
            dst_ref=dst,
            send_sem=send_sem,
            recv_sem=recv_sem,
            device_id={axis: target},
            device_id_type=MESH,
        )
        copy.start()
        pending.append(copy)
        return copy

    feats = proj.shape[0]
    piece = feats // npts
    sliced = piece % 16 == 0
    if sliced:
        piece_rows = pl.ds(pl.multiple_of(pts * piece, piece), piece)
    else:
        piece_rows = pl.ds(0, feats)
    p_copies = [
        send(
            proj.at[piece_rows],
            pfull.at[d, piece_rows],
            p_send.at[d],
            p_recv.at[d],
            "lst",
            (lst + d) % nlst,
        )
        for d in range(1, nlst)
    ]
    chunk = share // chunks
    t_copies = []
    for c in range(chunks):
        for d in range(1, nlst):
            z = (lst + d) % nlst
            t_copies.append(
                send(
                    tower.at[pl.ds(pl.multiple_of(z * share + c * chunk, chunk), chunk)],
                    full.at[c, d],
                    t_send.at[c, d],
                    t_recv.at[c, d],
                    "lst",
                    z,
                )
            )
    unit_rows = min(256, lists)

    @pl.loop(0, lists // unit_rows)
    def _(b):
        rows = pl.ds(pl.multiple_of(b * unit_rows, unit_rows), unit_rows)
        unit[rows, :] = rms_norm(cent[rows, :].astype(F32)).astype(BF16)
        lane_sums[rows, :] = jnp.zeros((unit_rows, LANES), F32)

    for copy in p_copies:
        copy.wait_recv()
    if sliced:
        q_copies = [
            send(
                pfull.at[pl.ds(1, nlst - 1), piece_rows],
                pfull.at[pl.ds(1, nlst - 1), piece_rows],
                q_send.at[d],
                q_recv.at[d],
                "pts",
                (pts + d) % npts,
            )
            for d in range(1, npts)
        ]

    if sliced:
        for copy in q_copies:
            copy.wait_recv()

    def hop(c, origin, left):
        side = 0 if left else 1
        return pltpu.make_async_remote_copy(
            src_ref=normed.at[c, origin],
            dst_ref=normed.at[c, origin],
            send_sem=n_send.at[side, c, origin],
            recv_sem=n_recv.at[c, origin],
            device_id={"lst": lst - 1 if left else lst + 1},
            device_id_type=MESH,
        )

    has_left = lst > 0
    has_right = lst < nlst - 1
    for c in range(chunks):
        hidden = jnp.dot(
            tower[pl.ds(pl.multiple_of(lst * share + c * chunk, chunk), chunk), :],
            proj[...],
            preferred_element_type=F32,
        )
        for d in range(1, nlst):
            t_copies[c * (nlst - 1) + d - 1].wait_recv()
            hidden += jnp.dot(full[c, d], pfull[d], preferred_element_type=F32)
        normed[c, lst] = rms_norm(hidden).astype(BF16)

        @pl.when(has_left)
        def _(c=c):
            hop(c, lst, True).start()

        @pl.when(has_right)
        def _(c=c):
            hop(c, lst, False).start()

    log2e = 1.0 / math.log(2.0)
    gain = log2e / (dp * temper)
    shift = -log2e / temper
    e_rows = min(1024, lists)
    step = min(256, chunk)

    def energy_of(c, origin):
        @pl.loop(0, lists // e_rows)
        def _(b):
            rows = pl.ds(pl.multiple_of(b * e_rows, e_rows), e_rows)
            sums = lane_sums[rows, :]
            for k in range(chunk // step):
                scores = lax.dot_general(
                    unit[rows, :],
                    normed[c, origin, k * step : (k + 1) * step, :],
                    (((1,), (1,)), ((), ())),
                    preferred_element_type=F32,
                )
                block = jnp.exp2(scores * gain + shift)
                at = pl.multiple_of(origin * share + c * chunk + k * step, step)
                energy[rows, pl.ds(at, step)] = block
                for m in range(step // LANES):
                    sums += block[:, m * LANES : (m + 1) * LANES]
            lane_sums[rows, :] = sums

    paired = jnp.minimum(lst, nlst - 1 - lst)
    for s in range(nlst):
        near = (s + 1) // 2
        far = s - paired
        in_pairs = lst - near if s % 2 else lst + near
        beyond = jnp.where(has_right & (lst < nlst - 1 - lst), lst + far, lst - far)
        origin = jnp.where(s <= 2 * paired, in_pairs, beyond) if s else lst
        for c in range(chunks):
            if s:
                hop(c, origin, True).wait_recv()

                @pl.when((origin < lst) & has_right)
                def _(c=c, origin=origin):
                    hop(c, origin, False).start()

                @pl.when((origin > lst) & has_left)
                def _(c=c, origin=origin):
                    hop(c, origin, True).start()

            energy_of(c, origin)

    for z in range(nlst):
        for c in range(chunks):

            @pl.when((z <= lst) & has_right)
            def _(c=c, z=z):
                hop(c, z, False).wait_send()

            @pl.when((z >= lst) & has_left)
            def _(c=c, z=z):
                hop(c, z, True).wait_send()

    def lane_dense(sums):
        return jnp.sum(sums.T, axis=0, keepdims=True)

    row_scale = None
    for sweep in range(ITERS):

        @pl.loop(0, list_blocks, unroll=4)
        def _(b, sweep=sweep, row_scale=row_scale):
            rows = pl.ds(pl.multiple_of(b * LANES, LANES), LANES)
            if sweep == 0:
                sums = lane_sums[rows, :]
            else:
                sums = energy[rows, 0:LANES] * row_scale[:, 0:LANES]
                for m in range(1, point_blocks):
                    lanes = slice(m * LANES, (m + 1) * LANES)
                    sums += energy[rows, lanes] * row_scale[:, lanes]
            col_sums[sweep, 0, pl.ds(b, 1), :] = lane_dense(sums)

        copies = [
            send(
                col_sums.at[sweep, 0],
                col_sums.at[sweep, d],
                c_send.at[sweep, d],
                c_recv.at[sweep, d],
                "pts",
                (pts + d) % npts,
            )
            for d in range(1, npts)
        ]
        for copy in copies:
            copy.wait_recv()
        total = col_sums[sweep, 0]
        for d in range(1, npts):
            total += col_sums[sweep, d]
        lane_sums[0:list_blocks, :] = balance / total

        def row_step(b, acc):
            rows = pl.ds(pl.multiple_of(b * LANES, LANES), LANES)
            wide = column_of(lane_sums[pl.ds(b, 1), :], LANES)
            if sweep == ITERS - 1:
                col_wide[rows, :] = wide
            parts = []
            for m in range(point_blocks):
                lanes = slice(m * LANES, (m + 1) * LANES)
                term = energy[rows, lanes] * wide
                parts.append(acc[m] + jnp.sum(term.reshape(LANES // 8, 8, LANES), axis=0))
            return tuple(parts)

        acc = lax.fori_loop(
            0,
            list_blocks,
            row_step,
            tuple(jnp.zeros((8, LANES), F32) for _ in range(point_blocks)),
            unroll=4,
        )
        per_slot = share // LANES
        for d in range(nlst):
            parts = [
                jnp.sum(acc[d * per_slot + m], axis=0, keepdims=True) for m in range(per_slot)
            ]
            row_sums[sweep, 0, d : d + 1, :] = jnp.concatenate(parts, axis=1)
        copies = [
            send(
                row_sums.at[sweep, 0],
                row_sums.at[sweep, d],
                r_send.at[sweep, d],
                r_recv.at[sweep, d],
                "lst",
                (lst + d) % nlst,
            )
            for d in range(1, nlst)
        ]
        for copy in copies:
            copy.wait_recv()
        total = row_sums[sweep, 0]
        for d in range(1, nlst):
            total += row_sums[sweep, d]
        scale = 1.0 / total
        row_scale = jnp.concatenate([scale[d : d + 1, :] for d in range(nlst)], axis=1)
    row_log[...] = jnp.log(scale)

    for m in range(point_blocks):
        d, k = divmod(m * LANES, share)
        wide = column_of(row_scale[:, m * LANES : (m + 1) * LANES], LANES)
        c, k = divmod(k, chunk)
        block = normed[c, d, k : k + LANES, :].astype(F32)
        for h in range(dp // LANES):
            lanes = slice(h * LANES, (h + 1) * LANES)
            scaled[m * LANES : (m + 1) * LANES, lanes] = (block[:, lanes] * wide).astype(BF16)

    tile = min(256, own)

    def partial_sums(owner, store):
        @pl.loop(0, own // tile)
        def _(t):
            rows = pl.ds(pl.multiple_of(owner * own + t * tile, tile), tile)
            store(
                pl.ds(pl.multiple_of(t * tile, tile), tile),
                jnp.dot(energy[rows, :].astype(BF16), scaled[...], preferred_element_type=F32),
            )

    partner = pts + 1 - 2 * core
    x_copies = []
    order = [d % chips for d in range(1, chips + 1)]
    for d in order:

        def to_pair(rows, values, d=d):
            pair_send[d, rows, :] = values.astype(BF16)

        partial_sums(((chip + d) % chips) * 2 + 1 - core, to_pair)
        x_copies.append(
            send(pair_send.at[d], pair_recv.at[d], x_send.at[d], x_recv.at[d], "pts", partner)
        )
    y_copies = []
    for n, d in enumerate(order):

        def to_mine(rows, values):
            mine[rows, :] = values

        owner = ((chip + d) % chips) * 2 + core
        partial_sums(owner, to_mine)
        x_copies[n].wait_recv()
        pair = mine[...] + pair_recv[d].astype(F32)
        if d:
            chip_send[d] = pair.astype(BF16)
            y_copies.append(
                send(chip_send.at[d], chip_recv.at[d], y_send.at[d], y_recv.at[d], "pts", owner)
            )
        else:
            mine[...] = pair
    for copy in y_copies:
        copy.wait_recv()
    sums = mine[...]
    for d in range(1, chips):
        sums += chip_recv[d].astype(F32)
    wide = col_wide[pl.ds(pl.multiple_of(pts * own, own), own), :]
    sums = sums * jnp.concatenate([wide] * (dp // LANES), axis=1)
    out[...] = rms_norm(sums)
    for copy in pending:
        copy.wait_send()


def on_device(npts, nlst, tower_out, projection, centroids):
    points = tower_out.shape[0]
    lists, dp = centroids.shape
    feats = tower_out.shape[1]
    share = points // nlst
    own = lists // npts
    chips = npts // 2
    chunks = 2 if share % (2 * LANES) == 0 else 1
    chunk = share // chunks
    vmem = pl.BlockSpec(memory_space=pltpu.VMEM)
    sem = pltpu.SemaphoreType.DMA
    centers, row_log = pl.pallas_call(
        functools.partial(kernel, npts, nlst, chunks),
        out_shape=(
            jax.ShapeDtypeStruct((own, dp), F32),
            jax.ShapeDtypeStruct((nlst, share), F32),
        ),
        in_specs=[vmem] * 3,
        out_specs=(vmem, vmem),
        scratch_shapes=[
            pltpu.VMEM((lists, points), F32),
            pltpu.VMEM((lists, dp), BF16),
            pltpu.VMEM((chunks, nlst, chunk, feats), BF16),
            pltpu.VMEM((nlst, feats, dp), BF16),
            pltpu.VMEM((chunks, nlst, chunk, dp), BF16),
            pltpu.VMEM((lists, LANES), F32),
            pltpu.VMEM((ITERS, npts, lists // LANES, LANES), F32),
            pltpu.VMEM((ITERS, nlst, nlst, share), F32),
            pltpu.VMEM((lists, LANES), F32),
            pltpu.VMEM((points, dp), BF16),
            pltpu.VMEM((chips, own, dp), BF16),
            pltpu.VMEM((chips, own, dp), BF16),
            pltpu.VMEM((chips, own, dp), BF16),
            pltpu.VMEM((chips, own, dp), BF16),
            pltpu.VMEM((own, dp), F32),
            sem((chunks, nlst)),
            sem((chunks, nlst)),
            sem((nlst,)),
            sem((nlst,)),
            sem((npts,)),
            sem((npts,)),
            sem((2, chunks, nlst)),
            sem((chunks, nlst)),
            sem((ITERS, npts)),
            sem((ITERS, npts)),
            sem((ITERS, nlst)),
            sem((ITERS, nlst)),
            sem((chips,)),
            sem((chips,)),
            sem((chips,)),
            sem((chips,)),
        ],
        compiler_params=pltpu.CompilerParams(
            collective_id=0, has_side_effects=True, vmem_limit_bytes=64000000
        ),
    )(tower_out, projection, centroids)
    return centers, row_log.reshape(points)


def solution(mesh):
    return jax.shard_map(
        functools.partial(on_device, mesh.shape["pts"], mesh.shape["lst"]),
        mesh=mesh,
        in_specs=(P("pts", "lst"), P("lst", None), P("lst", None)),
        out_specs=(P(("lst", "pts"), None), P("pts")),
        check_vma=False,
    )
```
